32 devices in a mesh: dp: 16 (over z, y, x), tensor: 2 (over core).
Axes of the slice: x: 2, y: 2, z: 4, core: 2. Of those that a mesh axis runs over, the one named last changes fastest.
Arguments:
- stream: float32 [16384, 768], P(('dp', 'tensor')), may hold values from -6 to 6
- cotangent: float32 [16384, 768], P(('dp', 'tensor')), may hold values from -6 to 6
- positions: int32 [16384], P('dp'), may hold values from -1 to 1023, as said below
- norm_gain: float32 [768], replicated, may hold values from 0.5 to 1.5
- w_gate: float32 [768, 1536], P('dp', 'tensor'), may hold values from -0.21875 to 0.21875
- w_inner: float32 [768, 1536], P('dp', 'tensor'), may hold values from -0.21875 to 0.21875
- w_state: float32 [768, 256], P('dp'), may hold values from -0.21875 to 0.21875
- w_step: float32 [768, 24], P('dp', 'tensor'), may hold values from -0.21875 to 0.21875
- conv_inner: float32 [5, 1536], P(None, 'tensor'), may hold values from -3 to 3
- conv_state: float32 [5, 256], replicated, may hold values from -3 to 3
- head_params: float32 [3, 24], P(None, 'tensor'), may hold values from -6 to 3, as said below
- gate_gain: float32 [1536], P('tensor'), may hold values from 0.5 to 1.5
- w_out: float32 [1536, 768], P('tensor', 'dp'), may hold values from -0.15625 to 0.15625
- moment_norm_gain: float32 [768], replicated, may hold values from -640 to 640
- moment_w_gate: float32 [768, 1536], P('dp', 'tensor'), may hold values from -192 to 192
- moment_w_inner: float32 [768, 1536], P('dp', 'tensor'), may hold values from -192 to 192
- moment_w_state: float32 [768, 256], P('dp', 'tensor'), may hold values from -192 to 192
- moment_w_step: float32 [768, 24], P('dp', 'tensor'), may hold values from -192 to 192
- moment_conv_inner: float32 [5, 1536], P(None, 'tensor'), may hold values from -640 to 640
- moment_conv_state: float32 [5, 256], replicated, may hold values from -640 to 640
- moment_head_params: float32 [3, 24], P(None, 'tensor'), may hold values from -640 to 640
- moment_gate_gain: float32 [1536], P('tensor'), may hold values from -640 to 640
- moment_w_out: float32 [1536, 768], P('tensor', 'dp'), may hold values from -192 to 192
Outputs:
- output: float32 [16384, 768], P(('dp', 'tensor'))
- d_stream: float32 [16384, 768], P(('dp', 'tensor'))
- grad_norm_gain: float32 [768], replicated
- grad_w_gate: float32 [768, 1536], P('dp', 'tensor')
- grad_w_inner: float32 [768, 1536], P('dp', 'tensor')
- grad_w_state: float32 [768, 256], P('dp', 'tensor')
- grad_w_step: float32 [768, 24], P('dp', 'tensor')
- grad_conv_inner: float32 [5, 1536], P(None, 'tensor')
- grad_conv_state: float32 [5, 256], replicated
- grad_head_params: float32 [3, 24], P(None, 'tensor')
- grad_gate_gain: float32 [1536], P('tensor')
- grad_w_out: float32 [1536, 768], P('tensor', 'dp')
- new_norm_gain: float32 [768], replicated
- new_w_gate: float32 [768, 1536], P('dp', 'tensor')
- new_w_inner: float32 [768, 1536], P('dp', 'tensor')
- new_w_state: float32 [768, 256], P('dp', 'tensor')
- new_w_step: float32 [768, 24], P('dp', 'tensor')
- new_conv_inner: float32 [5, 1536], P(None, 'tensor')
- new_conv_state: float32 [5, 256], replicated
- new_head_params: float32 [3, 24], P(None, 'tensor')
- new_gate_gain: float32 [1536], P('tensor')
- new_w_out: float32 [1536, 768], P('tensor', 'dp')
- new_moment_norm_gain: float32 [768], replicated
- new_moment_w_gate: float32 [768, 1536], P('dp', 'tensor')
- new_moment_w_inner: float32 [768, 1536], P('dp', 'tensor')
- new_moment_w_state: float32 [768, 256], P('dp', 'tensor')
- new_moment_w_step: float32 [768, 24], P('dp', 'tensor')
- new_moment_conv_inner: float32 [5, 1536], P(None, 'tensor')
- new_moment_conv_state: float32 [5, 256], replicated
- new_moment_head_params: float32 [3, 24], P(None, 'tensor')
- new_moment_gate_gain: float32 [1536], P('tensor')
- new_moment_w_out: float32 [1536, 768], P('tensor', 'dp')
The draws below stay inside these ranges and needn't reach their ends.
Inputs may be any that keep to these rules, and one draw needn't show every extreme that they name: `positions`: within each block of 1024 rows (one index of dp) an entry is the token's position in its sequence, 0 at a sequence's first token; every block starts a sequence at its first row, sequences stay inside a block, and -1 marks padding that only ends a block. `head_params`: row 0 step biases, row 1 logarithms of decay rates, row 2 skip gains.
All inputs are finite; a program needn't handle non-finite values.
Results may differ from the reference program's by a relative error of at most 0.023.
Values may be sent and summed in bfloat16 or wider, within the bound.
A program may use at most 128 MiB of HBM per device.

```python
import math
from functools import partial
import jax
import jax.numpy as jnp
from jax import lax

D = 768
INNER = 1536
HEADS = 24
STATE = 128
CONV = 4
BLOCK = 256
NS_STEPS = 5
TOK_DEV = 1024
TOKENS = 16384
N_TENSOR = 2


def draw_positions(key, part):
    blocks = TOKENS // TOK_DEV
    index = jnp.arange(TOK_DEV, dtype=jnp.int32)[None, :]
    block_id = jnp.arange(blocks, dtype=jnp.int32)[:, None]
    key_start, key_live = jax.random.split(key)
    starts = jax.random.randint(key_start, (blocks, TOK_DEV), 0, 96) == 0
    starts = starts & (block_id > 0) | (index == 0)
    marks = jnp.where(starts, index, 0)
    latest = lax.cummax(marks, axis=1)
    inside = index - latest
    shortfall = jax.random.randint(key_live, (blocks, 1), 0, TOK_DEV // 4)
    live_length = jnp.where(block_id == 0, TOK_DEV, TOK_DEV - 1 - shortfall)
    return jnp.where(index < live_length, inside, -1).reshape(TOKENS).astype(jnp.int32)


def draw_head_params(key, part):
    first, second, third = jax.random.split(jax.random.fold_in(key, 5), 3)
    bias = jax.random.uniform(first, (HEADS,), jnp.float32, -6.0, -2.5)
    rates = jax.random.uniform(second, (HEADS,), jnp.float32, math.log(0.5), math.log(16.0))
    skips = jax.random.uniform(third, (HEADS,), jnp.float32, 0.5, 1.5)
    return jnp.stack([bias, rates, skips]).astype(jnp.float32)


def levels(own_key, extent, cuts, smallest, largest):
    factor_of = 1.0
    for dim, shards_of in cuts:
        heights = jax.random.uniform(jax.random.fold_in(jax.random.fold_in(own_key, 6), dim), (shards_of,), jnp.float32, smallest / len(cuts), largest / len(cuts))
        factor_of = factor_of * jnp.repeat(jnp.exp(heights), extent[dim] // shards_of).reshape((-1,) + (1,) * (len(extent) - 1 - dim))
    return factor_of


def centred(key, shape, scale, limit, cuts=(), held_as=jnp.bfloat16):
    loudness = levels(key, shape, cuts, -0.22, 0.18) if cuts else 1.0
    values = jax.random.normal(key, shape, jnp.float32) * scale * loudness
    return jnp.minimum(jnp.maximum(values, -limit), limit).astype(held_as)


def setup_inputs(seed: int = 0) -> dict:
    splits = jax.random.split(jax.random.key(seed), 24)
    return {
        "stream": centred(splits[0], (TOKENS, D), 1.0, 6.0, ((0, 32),), jnp.float32),
        "cotangent": centred(splits[1], (TOKENS, D), 1.0, 6.0, ((0, 32),), jnp.float32),
        "positions": draw_positions(jax.random.fold_in(splits[23], 71), 0),
        "norm_gain": jnp.clip(1.0 + 0.1 * jax.random.normal(splits[3], (D,), jnp.float32), 0.5, 1.5),
        "w_gate": centred(splits[4], (D, INNER), D ** -0.5, 0.21875, ((0, 16), (1, 2)), jnp.float32),
        "w_inner": centred(splits[5], (D, INNER), D ** -0.5, 0.21875, ((0, 16), (1, 2)), jnp.float32),
        "w_state": centred(splits[6], (D, 2 * STATE), D ** -0.5, 0.21875, ((0, 16),), jnp.float32),
        "w_step": centred(splits[7], (D, HEADS), D ** -0.5, 0.21875, ((0, 16), (1, 2)), jnp.float32),
        "conv_inner": centred(splits[8], (CONV + 1, INNER), 0.5, 3.0, ((1, 2),), jnp.float32),
        "conv_state": centred(splits[9], (CONV + 1, 2 * STATE), 0.5, 3.0, (), jnp.float32),
        "head_params": draw_head_params(jax.random.fold_in(splits[23], 71), 0),
        "gate_gain": jnp.clip(1.0 + 0.1 * jax.random.normal(splits[11], (INNER,), jnp.float32), 0.5, 1.5),
        "w_out": centred(splits[12], (INNER, D), INNER ** -0.5, 0.15625, ((0, 2), (1, 16)), jnp.float32),
        "moment_norm_gain": centred(splits[13], (D,), 100.0, 640.0, (), jnp.float32),
        "moment_w_gate": centred(splits[14], (D, INNER), 30.0, 192.0, ((0, 16), (1, 2)), jnp.float32),
        "moment_w_inner": centred(splits[15], (D, INNER), 30.0, 192.0, ((0, 16), (1, 2)), jnp.float32),
        "moment_w_state": centred(splits[16], (D, 2 * STATE), 30.0, 192.0, ((0, 16), (1, 2)), jnp.float32),
        "moment_w_step": centred(splits[17], (D, HEADS), 30.0, 192.0, ((0, 16), (1, 2)), jnp.float32),
        "moment_conv_inner": centred(splits[18], (CONV + 1, INNER), 100.0, 640.0, ((1, 2),), jnp.float32),
        "moment_conv_state": centred(splits[19], (CONV + 1, 2 * STATE), 100.0, 640.0, (), jnp.float32),
        "moment_head_params": centred(splits[20], (3, HEADS), 100.0, 640.0, ((1, 2),), jnp.float32),
        "moment_gate_gain": centred(splits[21], (INNER,), 100.0, 640.0, ((0, 2),), jnp.float32),
        "moment_w_out": centred(splits[22], (INNER, D), 30.0, 192.0, ((0, 2), (1, 16)), jnp.float32),
    }


EPS = 1e-05
NS_A = 3.4445
NS_B = -4.775
NS_C = 2.0315
MU_MAT = 0.95
MU_VEC = 0.9
LR_MAT = 0.3
LR_VEC = 0.001
HIGH = lax.Precision.HIGHEST

def silu_slope(value):
    sig = jax.nn.sigmoid(value)
    return sig * (1.0 + value * (1.0 - sig))

def contract_rows(left, right):
    return lax.dot_general(left, right, (((0,), (0,)), ((), ())), preferred_element_type=jnp.float32)

def times_transpose(left, right):
    return lax.dot_general(left, right, (((1,), (1,)), ((), ())), preferred_element_type=jnp.float32)

def causal_conv(signal, taps, positions):
    length = signal.shape[0]
    reach = taps.shape[0] - 1
    total = jnp.zeros_like(signal) + taps[reach]
    for lag_step in range(reach):
        moved = jnp.pad(signal, ((lag_step, 0), (0, 0)))[:length]
        total = total + jnp.where((positions >= lag_step)[:, None], moved * taps[lag_step], 0.0)
    return jax.nn.silu(total)

def mixer_core(inner_pre, state_pre, step_pre, conv_inner, conv_state, head_params, positions):
    length = inner_pre.shape[0]
    heads = step_pre.shape[1]
    head_size = inner_pre.shape[1] // heads
    states = state_pre.shape[1] // 2
    blocks = length // BLOCK
    inner_act = causal_conv(inner_pre, conv_inner, positions).reshape(blocks, BLOCK, heads, head_size)
    state_act = causal_conv(state_pre, conv_state, positions)
    input_map = state_act[:, :states].reshape(blocks, BLOCK, states)
    output_map = state_act[:, states:].reshape(blocks, BLOCK, states)
    step_size = jax.nn.softplus(step_pre + head_params[0])
    log_decay = (step_size * -jnp.exp(head_params[1])).reshape(blocks, BLOCK, heads)
    step_size = step_size.reshape(blocks, BLOCK, heads)
    resets = (positions <= 0).astype(jnp.float32).reshape(blocks, BLOCK)
    cumulative = jnp.cumsum(log_decay, axis=1)
    seen = jnp.cumsum(resets, axis=1)
    order = jnp.arange(BLOCK)
    linked = (seen[:, :, None] == seen[:, None, :]) & (order[:, None] >= order[None, :])[None]
    linked_heads = linked[..., None]
    spacing = cumulative[:, :, None, :] - cumulative[:, None, :, :]
    decay = jnp.where(linked_heads, jnp.exp(jnp.where(linked_heads, spacing, 0.0)), 0.0)
    scores = jnp.einsum('cin,cjn->cij', output_map, input_map, precision=HIGH)
    mixing = scores[..., None] * decay * step_size[:, None, :, :]
    within = jnp.einsum('cijh,cjhp->cihp', mixing, inner_act, precision=HIGH)
    tail_linked = (seen[:, -1:] == seen)[..., None]
    tail = jnp.where(tail_linked, jnp.exp(jnp.where(tail_linked, cumulative[:, -1:, :] - cumulative, 0.0)), 0.0) * step_size
    own_state = jnp.einsum('cjh,cjhp,cjn->chpn', tail, inner_act, input_map, precision=HIGH)
    carry_rate = jnp.exp(cumulative[:, -1, :]) * (seen[:, -1] == 0).astype(jnp.float32)[:, None]

    def advance(state, inputs):
        rate, fresh_state = inputs
        return (rate[:, None, None] * state + fresh_state, state)
    _, entering = lax.scan(advance, jnp.zeros((heads, head_size, states), jnp.float32), (carry_rate, own_state))
    fresh = (seen == 0)[..., None]
    carry_in = jnp.where(fresh, jnp.exp(cumulative), 0.0)
    across = jnp.einsum('cin,chpn->cihp', output_map, entering, precision=HIGH) * carry_in[..., None]
    result = within + across + head_params[2][None, None, :, None] * inner_act
    return result.reshape(length, heads * head_size)

def layer_pass(stream, cotangent, positions, params):
    norm_gain, full_gate, full_inner, full_state, full_step, conv_inner, conv_state, head_params, gate_gain, full_out = params
    inv_first = lax.rsqrt(lax.optimization_barrier(jnp.mean(stream * stream, axis=1, keepdims=True)) + EPS)
    normed = (stream * inv_first * norm_gain).astype(jnp.bfloat16)
    gate_pre = jnp.dot(normed, full_gate, preferred_element_type=jnp.float32)
    inner_pre = jnp.dot(normed, full_inner, preferred_element_type=jnp.float32)
    state_pre = jnp.dot(normed, full_state, preferred_element_type=jnp.float32)
    step_pre = jnp.dot(normed, full_step, preferred_element_type=jnp.float32)
    alive = (positions >= 0).astype(jnp.float32)[:, None]
    scanned, core_back = jax.vjp(partial(mixer_core, positions=positions), inner_pre, state_pre, step_pre, conv_inner, conv_state, head_params)
    gate_act = jax.nn.silu(gate_pre)
    gated = scanned * gate_act
    inv_second = lax.rsqrt(lax.optimization_barrier(jnp.sum(gated * gated, axis=1, keepdims=True)) / INNER + EPS)
    normed_out = (gated * inv_second * gate_gain * alive).astype(jnp.bfloat16)
    output = stream + jnp.dot(normed_out, full_out, preferred_element_type=jnp.float32)
    cot_low = cotangent.astype(jnp.bfloat16)
    d_normed_out = times_transpose(cot_low, full_out)
    grad_out = contract_rows(normed_out, cot_low)
    scaled = d_normed_out * gate_gain * alive
    grad_gate_gain = lax.optimization_barrier(jnp.sum(d_normed_out * gated * inv_second * alive, axis=0))
    cross_sum = lax.optimization_barrier(jnp.sum(scaled * gated, axis=1, keepdims=True))
    d_gated = inv_second * scaled - gated * inv_second ** 3 * (cross_sum / INNER)
    d_gate_pre = (d_gated * scanned * silu_slope(gate_pre)).astype(jnp.bfloat16)
    d_inner, d_state, d_step, grad_conv_inner, grad_conv_state, grad_head = core_back(d_gated * gate_act)
    d_inner_low = d_inner.astype(jnp.bfloat16)
    d_state_low = d_state.astype(jnp.bfloat16)
    d_step_low = d_step.astype(jnp.bfloat16)
    d_normed = times_transpose(d_gate_pre, full_gate) + times_transpose(d_inner_low, full_inner)
    d_normed = d_normed + times_transpose(d_state_low, full_state) + times_transpose(d_step_low, full_step)
    grad_norm = lax.optimization_barrier(jnp.sum(d_normed * stream * inv_first, axis=0))
    weighted = d_normed * norm_gain
    d_stream = cotangent + inv_first * weighted - stream * inv_first ** 3 * lax.optimization_barrier(jnp.mean(weighted * stream, axis=1, keepdims=True))
    grads = (grad_norm, contract_rows(normed, d_gate_pre), contract_rows(normed, d_inner_low), contract_rows(normed, d_state_low), contract_rows(normed, d_step_low), grad_conv_inner, grad_conv_state, grad_head, grad_gate_gain, grad_out)
    return (output, d_stream, grads)

def gram_groups(low, groups):
    rows = low.shape[0]
    width = low.shape[1] // groups
    pieces = low.astype(jnp.float32).reshape(rows, groups, width)
    terms = jnp.einsum('rgc,sgc->grs', pieces, pieces, precision=HIGH)
    rounded = lax.optimization_barrier(terms.astype(jnp.bfloat16))
    return lax.optimization_barrier(jnp.sum(rounded.astype(jnp.float32), axis=0))

def orthogonalize(matrix, groups):
    first = gram_groups(matrix.astype(jnp.bfloat16), groups)
    scale = jnp.sqrt(jnp.trace(first)) + 1e-07
    current = (matrix / scale).astype(jnp.bfloat16)
    gram = (first / (scale * scale)).astype(jnp.bfloat16)
    for turn in range(NS_STEPS):
        if turn > 0:
            gram = gram_groups(current, groups).astype(jnp.bfloat16)
        applied = jnp.dot(gram, current, preferred_element_type=jnp.float32)
        twice = jnp.dot(gram, applied.astype(jnp.bfloat16), preferred_element_type=jnp.float32)
        current = (NS_A * current.astype(jnp.float32) + NS_B * applied + NS_C * twice).astype(jnp.bfloat16)
    return current.astype(jnp.float32)

def widen(matrix, groups):
    rows = matrix.shape[0]
    width = matrix.shape[1] // groups
    room = INNER // groups
    return jnp.pad(matrix.reshape(rows, groups, width), ((0, 0), (0, 0), (0, room - width))).reshape(rows, groups * room)

def narrow(matrix, groups, width):
    rows = matrix.shape[0]
    room = matrix.shape[1] // groups
    return matrix.reshape(rows, groups, room)[:, :, :width].reshape(rows, groups * width)

def spread(rows, cols):
    return math.sqrt(max(1.0, rows / cols))

def reference(stream, cotangent, positions, norm_gain, w_gate, w_inner, w_state, w_step, conv_inner, conv_state, head_params, gate_gain, w_out, moment_norm_gain, moment_w_gate, moment_w_inner, moment_w_state, moment_w_step, moment_conv_inner, moment_conv_state, moment_head_params, moment_gate_gain, moment_w_out):
    params = (norm_gain, w_gate.astype(jnp.bfloat16), w_inner.astype(jnp.bfloat16), w_state.astype(jnp.bfloat16), w_step.astype(jnp.bfloat16), conv_inner, conv_state, head_params, gate_gain, w_out.astype(jnp.bfloat16))
    initials = (norm_gain, w_gate, w_inner, w_state, w_step, conv_inner, conv_state, head_params, gate_gain, w_out)
    init = tuple((jnp.zeros(item.shape, jnp.float32) for item in initials))
    blocks = stream.shape[0] // TOK_DEV

    def one_block(totals, data):
        rows, cots, where_pos = data
        output, d_rows, grads = layer_pass(rows, cots, where_pos, params)
        return (tuple((first + second for first, second in zip(totals, grads))), (output, d_rows))
    grads, (outputs, d_streams) = lax.scan(one_block, init, (stream.reshape(blocks, TOK_DEV, D), cotangent.reshape(blocks, TOK_DEV, D), positions.reshape(blocks, TOK_DEV)))
    g_norm, g_gate, g_inner, g_state, g_step, g_conv_inner, g_conv_state, g_head, g_gate_gain, g_out = grads
    groups = N_TENSOR
    m_gate = MU_MAT * moment_w_gate + g_gate
    m_inner = MU_MAT * moment_w_inner + g_inner
    m_state = MU_MAT * moment_w_state + g_state
    m_step = MU_MAT * moment_w_step + g_step
    m_out = MU_MAT * moment_w_out + g_out
    new_gate = w_gate - LR_MAT * spread(D, INNER) * orthogonalize(m_gate, groups)
    new_inner = w_inner - LR_MAT * spread(D, INNER) * orthogonalize(m_inner, groups)
    new_out = w_out - LR_MAT * spread(INNER, D) * orthogonalize(m_out.T, groups).T
    new_step = w_step - LR_MAT * spread(D, HEADS) * narrow(orthogonalize(widen(m_step, groups), groups), groups, HEADS // groups)
    new_state = w_state - LR_MAT * spread(D, 2 * STATE) * narrow(orthogonalize(widen(m_state, groups), groups), groups, 2 * STATE // groups)
    m_norm = MU_VEC * moment_norm_gain + g_norm
    m_conv_inner = MU_VEC * moment_conv_inner + g_conv_inner
    m_conv_state = MU_VEC * moment_conv_state + g_conv_state
    m_head = MU_VEC * moment_head_params + g_head
    m_gate_gain = MU_VEC * moment_gate_gain + g_gate_gain
    return (outputs.reshape(stream.shape), d_streams.reshape(stream.shape), g_norm, g_gate, g_inner, g_state, g_step, g_conv_inner, g_conv_state, g_head, g_gate_gain, g_out, norm_gain - LR_VEC * m_norm, new_gate, new_inner, new_state, new_step, conv_inner - LR_VEC * m_conv_inner, conv_state - LR_VEC * m_conv_state, head_params - LR_VEC * m_head, gate_gain - LR_VEC * m_gate_gain, new_out, m_norm, m_gate, m_inner, m_state, m_step, m_conv_inner, m_conv_state, m_head, m_gate_gain, m_out)
```

```python
from functools import partial
import math

import jax
import jax.numpy as jnp
from jax import lax
from jax.sharding import PartitionSpec as P

D = 768
INNER = 1536
HEADS = 24
STATE = 128
BLOCK = 256
NS_STEPS = 5


EPS = 1e-05
NS_A = 3.4445
NS_B = -4.775
NS_C = 2.0315
MU_MAT = 0.95
MU_VEC = 0.9
LR_MAT = 0.3
LR_VEC = 0.001
HIGH = lax.Precision.HIGHEST
CORE = lax.Precision.DEFAULT


def silu_slope(value):
    sig = jax.nn.sigmoid(value)
    return sig * (1.0 + value * (1.0 - sig))


def contract_rows(left, right):
    return lax.dot_general(
        left, right, (((0,), (0,)), ((), ())), preferred_element_type=jnp.float32
    )


def times_transpose(left, right):
    return lax.dot_general(
        left, right, (((1,), (1,)), ((), ())), preferred_element_type=jnp.float32
    )


def causal_conv(signal, taps, positions):
    length = signal.shape[0]
    reach = taps.shape[0] - 1
    total = jnp.zeros_like(signal) + taps[reach]
    for lag_step in range(reach):
        moved = jnp.pad(signal, ((lag_step, 0), (0, 0)))[:length]
        total = total + jnp.where((positions >= lag_step)[:, None], moved * taps[lag_step], 0.0)
    return jax.nn.silu(total)


def mixer_core(inner_pre, state_pre, step_pre, conv_inner, conv_state, head_params, positions, precision=HIGH):
    length = inner_pre.shape[0]
    heads = step_pre.shape[1]
    head_size = inner_pre.shape[1] // heads
    states = state_pre.shape[1] // 2
    blocks = length // BLOCK
    inner_act = causal_conv(inner_pre, conv_inner, positions).reshape(
        blocks, BLOCK, heads, head_size
    )
    state_act = causal_conv(state_pre, conv_state, positions)
    input_map = state_act[:, :states].reshape(blocks, BLOCK, states)
    output_map = state_act[:, states:].reshape(blocks, BLOCK, states)
    step_size = jax.nn.softplus(step_pre + head_params[0])
    log_decay = (step_size * -jnp.exp(head_params[1])).reshape(blocks, BLOCK, heads)
    step_size = step_size.reshape(blocks, BLOCK, heads)
    resets = (positions <= 0).astype(jnp.float32).reshape(blocks, BLOCK)
    cumulative = jnp.cumsum(log_decay, axis=1)
    seen = jnp.cumsum(resets, axis=1)
    order = jnp.arange(BLOCK)
    linked = (seen[:, :, None] == seen[:, None, :]) & (order[:, None] >= order[None, :])[None]
    linked_heads = linked[..., None]
    spacing = cumulative[:, :, None, :] - cumulative[:, None, :, :]
    decay = jnp.where(linked_heads, jnp.exp(jnp.where(linked_heads, spacing, 0.0)), 0.0)
    scores = jnp.einsum("cin,cjn->cij", output_map, input_map, precision=precision)
    mixing = scores[..., None] * decay * step_size[:, None, :, :]
    within = jnp.einsum("cijh,cjhp->cihp", mixing, inner_act, precision=precision)
    tail_linked = (seen[:, -1:] == seen)[..., None]
    tail = (
        jnp.where(
            tail_linked,
            jnp.exp(jnp.where(tail_linked, cumulative[:, -1:, :] - cumulative, 0.0)),
            0.0,
        )
        * step_size
    )
    own_state = jnp.einsum("cjh,cjhp,cjn->chpn", tail, inner_act, input_map, precision=precision)
    carry_rate = jnp.exp(cumulative[:, -1, :]) * (seen[:, -1] == 0).astype(jnp.float32)[:, None]

    def advance(state, inputs):
        rate, fresh_state = inputs
        return (rate[:, None, None] * state + fresh_state, state)

    _, entering = lax.scan(
        advance, jnp.zeros((heads, head_size, states), jnp.float32), (carry_rate, own_state)
    )
    fresh = (seen == 0)[..., None]
    carry_in = jnp.where(fresh, jnp.exp(cumulative), 0.0)
    across = (
        jnp.einsum("cin,chpn->cihp", output_map, entering, precision=precision) * carry_in[..., None]
    )
    result = within + across + head_params[2][None, None, :, None] * inner_act
    return result.reshape(length, heads * head_size)


def gram_total(low):
    return lax.psum(
        jnp.dot(low, low.T, preferred_element_type=jnp.float32).astype(jnp.bfloat16), "tensor"
    ).astype(jnp.float32)


def orthogonalize(matrix):
    first = gram_total(matrix.astype(jnp.bfloat16))
    scale = jnp.sqrt(jnp.trace(first)) + 1e-07
    current = (matrix / scale).astype(jnp.bfloat16)
    gram = (first / (scale * scale)).astype(jnp.bfloat16)
    for turn in range(NS_STEPS):
        if turn > 0:
            gram = gram_total(current).astype(jnp.bfloat16)
        applied = jnp.dot(gram, current, preferred_element_type=jnp.float32)
        twice = jnp.dot(gram, applied.astype(jnp.bfloat16), preferred_element_type=jnp.float32)
        current = (NS_A * current.astype(jnp.float32) + NS_B * applied + NS_C * twice).astype(
            jnp.bfloat16
        )
    return current.astype(jnp.float32)


def spread(rows, cols):
    return math.sqrt(max(1.0, rows / cols))


def shards(
    stream,
    cotangent,
    positions,
    norm_gain,
    w_gate,
    w_inner,
    w_state,
    w_step,
    conv_inner,
    conv_state,
    head_params,
    gate_gain,
    w_out,
    moment_norm_gain,
    moment_w_gate,
    moment_w_inner,
    moment_w_state,
    moment_w_step,
    moment_conv_inner,
    moment_conv_state,
    moment_head_params,
    moment_gate_gain,
    moment_w_out,
):
    dp_count = lax.axis_size("dp")
    inv_first = lax.rsqrt(jnp.mean(stream * stream, axis=1, keepdims=True) + EPS)
    normed = (stream * inv_first * norm_gain).astype(jnp.bfloat16)
    token_rows, cotangent_rows = (
        lax.all_gather(normed, "tensor", axis=0, tiled=True),
        lax.all_gather(cotangent.astype(jnp.bfloat16), "tensor", axis=0, tiled=True),
    )
    local_weights = (
        w_gate.astype(jnp.bfloat16),
        w_inner.astype(jnp.bfloat16),
        w_step.astype(jnp.bfloat16),
        w_state.astype(jnp.bfloat16),
        w_out.astype(jnp.bfloat16),
    )
    full_gate, full_inner, full_step, full_state, full_out = (
        lax.all_gather(local_weights[0], "dp", axis=0, tiled=True),
        lax.all_gather(local_weights[1], "dp", axis=0, tiled=True),
        lax.all_gather(local_weights[2], "dp", axis=0, tiled=True),
        lax.all_gather(local_weights[3], "dp", axis=0, tiled=True),
        lax.all_gather(local_weights[4], "dp", axis=1, tiled=True),
    )
    gate_pre = jnp.dot(token_rows, full_gate, preferred_element_type=jnp.float32)
    inner_pre = jnp.dot(token_rows, full_inner, preferred_element_type=jnp.float32)
    state_pre = jnp.dot(token_rows, full_state, preferred_element_type=jnp.float32)
    step_pre = jnp.dot(token_rows, full_step, preferred_element_type=jnp.float32)
    alive = (positions >= 0).astype(jnp.float32)[:, None]
    scanned, core_back = jax.vjp(
        partial(mixer_core, positions=positions),
        inner_pre,
        state_pre,
        step_pre,
        conv_inner,
        conv_state,
        head_params,
    )
    gate_act = jax.nn.silu(gate_pre)
    gated = scanned * gate_act
    square_sum = lax.psum(jnp.sum(gated * gated, axis=1), "tensor")
    inv_second = lax.rsqrt(square_sum / INNER + EPS)[:, None]
    normed_out = (gated * inv_second * gate_gain * alive).astype(jnp.bfloat16)
    mixed = lax.psum_scatter(
        jnp.dot(normed_out, full_out, preferred_element_type=jnp.float32).astype(jnp.bfloat16),
        "tensor",
        scatter_dimension=0,
        tiled=True,
    ).astype(jnp.float32)
    output = stream + mixed
    d_normed_out = times_transpose(cotangent_rows, full_out)
    grad_out_part = contract_rows(normed_out, cotangent_rows)
    scaled = d_normed_out * gate_gain * alive
    grad_gate_part = jnp.sum(d_normed_out * gated * inv_second * alive, axis=0)
    cross_sum = lax.psum(jnp.sum(scaled * gated, axis=1), "tensor")
    d_gated = inv_second * scaled - gated * inv_second**3 * (cross_sum / INNER)[:, None]
    d_gate_pre = (d_gated * scanned * silu_slope(gate_pre)).astype(jnp.bfloat16)
    d_inner, d_state_part, d_step, grad_conv_inner_part, grad_conv_state_part, grad_head_part = (
        core_back(d_gated * gate_act)
    )
    d_state_cols = lax.psum_scatter(
        d_state_part.astype(jnp.bfloat16), "tensor", scatter_dimension=1, tiled=True
    ).astype(jnp.float32)
    d_inner_low = d_inner.astype(jnp.bfloat16)
    d_state_low = d_state_cols.astype(jnp.bfloat16)
    d_step_low = d_step.astype(jnp.bfloat16)
    col_width = d_state_cols.shape[1]
    col_first = lax.axis_index("tensor") * col_width
    state_cols = lax.dynamic_slice_in_dim(full_state, col_first, col_width, 1)
    total = times_transpose(d_gate_pre, full_gate)
    total = total + times_transpose(d_inner_low, full_inner)
    total = total + times_transpose(d_state_low, state_cols)
    d_normed = lax.psum_scatter(
        (total + times_transpose(d_step_low, full_step)).astype(jnp.bfloat16),
        "tensor",
        scatter_dimension=0,
        tiled=True,
    ).astype(jnp.float32)
    grad_gate_w, grad_inner_w, grad_state_w, grad_step_w, grad_out_w = (
        lax.psum_scatter(
            contract_rows(token_rows, d_gate_pre).astype(jnp.bfloat16),
            "dp",
            scatter_dimension=0,
            tiled=True,
        ).astype(jnp.float32),
        lax.psum_scatter(
            contract_rows(token_rows, d_inner_low).astype(jnp.bfloat16),
            "dp",
            scatter_dimension=0,
            tiled=True,
        ).astype(jnp.float32),
        lax.psum_scatter(
            contract_rows(token_rows, d_state_low).astype(jnp.bfloat16),
            "dp",
            scatter_dimension=0,
            tiled=True,
        ).astype(jnp.float32),
        lax.psum_scatter(
            contract_rows(token_rows, d_step_low).astype(jnp.bfloat16),
            "dp",
            scatter_dimension=0,
            tiled=True,
        ).astype(jnp.float32),
        lax.psum_scatter(
            grad_out_part.astype(jnp.bfloat16), "dp", scatter_dimension=1, tiled=True
        ).astype(jnp.float32),
    )
    grad_norm_part = jnp.sum(d_normed * stream * inv_first, axis=0)
    weighted = d_normed * norm_gain
    d_stream = (
        cotangent
        + inv_first * weighted
        - stream * inv_first**3 * jnp.mean(weighted * stream, axis=1, keepdims=True)
    )
    grad_conv_inner, grad_gate_gain, grad_head = lax.psum(
        (grad_conv_inner_part, grad_gate_part, grad_head_part), "dp"
    )
    grad_conv_state, grad_norm = lax.psum((grad_conv_state_part, grad_norm_part), ("dp", "tensor"))
    m_gate = MU_MAT * moment_w_gate + grad_gate_w
    m_inner = MU_MAT * moment_w_inner + grad_inner_w
    m_state = MU_MAT * moment_w_state + grad_state_w
    m_step = MU_MAT * moment_w_step + grad_step_w
    m_out = MU_MAT * moment_w_out + grad_out_w
    room = w_gate.shape[1]
    shard_rows = w_gate.shape[0]
    stacked = jnp.stack(
        [
            m_gate,
            m_inner,
            m_out.T,
            jnp.pad(m_step, ((0, 0), (0, room - m_step.shape[1]))),
            jnp.pad(m_state, ((0, 0), (0, room - m_state.shape[1]))),
        ]
    )
    matrix_count = stacked.shape[0]
    owner_index = jnp.arange(matrix_count, dtype=jnp.int32) * dp_count // matrix_count
    select = (owner_index[None, :] == jnp.arange(dp_count, dtype=jnp.int32)[:, None]).astype(
        jnp.float32
    )
    outgoing = jnp.einsum("jk,krc->jrc", select, stacked, precision=HIGH)
    owned = (
        lax.all_to_all(outgoing.astype(jnp.bfloat16), "dp", split_axis=0, concat_axis=0, tiled=True)
        .astype(outgoing.dtype)
        .reshape(dp_count * shard_rows, room)
    )
    ortho = orthogonalize(owned)
    returned = lax.all_to_all(
        ortho.reshape(dp_count, shard_rows, room).astype(jnp.bfloat16),
        "dp",
        split_axis=0,
        concat_axis=0,
        tiled=True,
    ).astype(jnp.float32)
    mine = jnp.einsum("jk,jrc->krc", select, returned, precision=HIGH)
    new_gate = w_gate - LR_MAT * spread(D, INNER) * mine[0]
    new_inner = w_inner - LR_MAT * spread(D, INNER) * mine[1]
    new_out = w_out - LR_MAT * spread(INNER, D) * mine[2].T
    new_step = w_step - LR_MAT * spread(D, HEADS) * mine[3][:, : w_step.shape[1]]
    state_slice = lax.dynamic_slice_in_dim(w_state, col_first, col_width, 1)
    new_state = state_slice - LR_MAT * spread(D, 2 * STATE) * mine[4][:, :col_width]
    m_norm = MU_VEC * moment_norm_gain + grad_norm
    m_conv_inner = MU_VEC * moment_conv_inner + grad_conv_inner
    m_conv_state = MU_VEC * moment_conv_state + grad_conv_state
    m_head = MU_VEC * moment_head_params + grad_head
    m_gate_gain = MU_VEC * moment_gate_gain + grad_gate_gain
    return (
        output,
        d_stream,
        grad_norm,
        grad_gate_w,
        grad_inner_w,
        grad_state_w,
        grad_step_w,
        grad_conv_inner,
        grad_conv_state,
        grad_head,
        grad_gate_gain,
        grad_out_w,
        norm_gain - LR_VEC * m_norm,
        new_gate,
        new_inner,
        new_state,
        new_step,
        conv_inner - LR_VEC * m_conv_inner,
        conv_state - LR_VEC * m_conv_state,
        head_params - LR_VEC * m_head,
        gate_gain - LR_VEC * m_gate_gain,
        new_out,
        m_norm,
        m_gate,
        m_inner,
        m_state,
        m_step,
        m_conv_inner,
        m_conv_state,
        m_head,
        m_gate_gain,
        m_out,
    )


def exchange(value, bit):
    count = lax.axis_size("dp")
    return lax.ppermute(value, "dp", [(i, i ^ bit) for i in range(count)])


def swap(value):
    return lax.ppermute(value, "tensor", [(0, 1), (1, 0)])


def bit_of(bit):
    return (lax.axis_index("dp") // bit) % 2


def join(kept, received, mine, axis):
    first = jnp.where(mine == 0, kept, received)
    second = jnp.where(mine == 0, received, kept)
    return jnp.concatenate([first, second], axis=axis)


AXIS_OF = {8: 0, 4: 1, 2: 2, 1: 3}


def spread_rows(held, order):
    for bit in order:
        held = join(held, exchange(held, bit), bit_of(bit), AXIS_OF[bit])
    return held


def gather_rows(block, order):
    rows, cols = block.shape
    held = spread_rows(block.reshape(1, 1, 1, 1, rows, cols), order)
    return held.reshape(16 * rows, cols)


def scatter_rows(part, order):
    rows, cols = part.shape
    held = part.reshape(2, 2, 2, 2, rows // 16, cols)
    for bit in order:
        axis = AXIS_OF[bit]
        mine = bit_of(bit)
        send = lax.dynamic_index_in_dim(held, 1 - mine, axis, keepdims=True)
        keep = lax.dynamic_index_in_dim(held, mine, axis, keepdims=True)
        total = keep.astype(jnp.float32) + exchange(send.astype(jnp.bfloat16), bit).astype(
            jnp.float32
        )
        held = total.astype(jnp.bfloat16) if bit != order[-1] else total
    return held.reshape(rows // 16, cols)


def pair_gather(block):
    return join(block, swap(block), lax.axis_index("tensor"), 0)


def pair_scatter(part, axis):
    mine = lax.axis_index("tensor")
    width = part.shape[axis] // 2
    keep = lax.dynamic_slice_in_dim(part, mine * width, width, axis)
    send = lax.dynamic_slice_in_dim(part, (1 - mine) * width, width, axis)
    return keep.astype(jnp.float32) + swap(send.astype(jnp.bfloat16)).astype(jnp.float32)


def pad_cols(value, width):
    return jnp.pad(value, ((0, 0), (0, width - value.shape[1])))


def to_owner(tasks):
    _, rows, cols = tasks.shape
    across, along = bit_of(1), bit_of(2)
    held = tasks.reshape(2, 2, rows, cols)
    send = lax.dynamic_index_in_dim(held, 1 - across, 1)
    keep = lax.dynamic_index_in_dim(held, across, 1)
    held = join(keep, exchange(send, 1), across, 1)
    send = lax.dynamic_index_in_dim(held, 1 - along, 0)
    keep = lax.dynamic_index_in_dim(held, along, 0)
    held = join(keep, exchange(send, 2), along, 0)
    held = spread_rows(held.reshape(1, 1, 2, 2, rows, cols), (8, 4))
    return held.reshape(16 * rows, cols)


def from_owner(matrix):
    rows, cols = matrix.shape[0] // 16, matrix.shape[1]
    across, along = bit_of(1), bit_of(2)
    plane = lax.dynamic_index_in_dim(
        matrix.reshape(4, 2, 2, rows, cols), lax.axis_index("dp") // 4, 0, keepdims=False
    )
    send = lax.dynamic_index_in_dim(plane, 1 - along, 0)
    keep = lax.dynamic_index_in_dim(plane, along, 0)
    held = join(keep, exchange(send, 2), along, 0)
    send = lax.dynamic_index_in_dim(held, 1 - across, 1)
    keep = lax.dynamic_index_in_dim(held, across, 1)
    return join(keep, exchange(send, 1), across, 1).reshape(4, rows, cols)


def orthogonal_half(own, state_width):
    width = own.shape[1]
    small = lax.axis_index("dp") % 4 == 3
    full = jnp.concatenate([own, swap(own)], axis=1)
    col = jnp.arange(2 * width)[None, :] % width
    keep = (col < state_width) == (lax.axis_index("tensor") == 0)
    full = jnp.where(small & ~keep, jnp.zeros_like(full), full)
    first = times_transpose(full, full)
    scale = jnp.sqrt(jnp.sum(jnp.square(full.astype(jnp.float32)))) + 1e-07
    current = (full.astype(jnp.float32) / scale).astype(jnp.bfloat16)
    gram = (first / (scale * scale)).astype(jnp.bfloat16)
    for turn in range(NS_STEPS):
        if turn > 0:
            gram = times_transpose(current, current).astype(jnp.bfloat16)
        square = jnp.dot(gram, gram, preferred_element_type=jnp.float32)
        mix = (NS_B * gram.astype(jnp.float32) + NS_C * square).astype(jnp.bfloat16)
        if turn == NS_STEPS - 1:
            current = current[:, : width + 2 * state_width]
        current = (
            NS_A * current.astype(jnp.float32)
            + jnp.dot(mix, current, preferred_element_type=jnp.float32)
        ).astype(jnp.bfloat16)
    half, lent = current[:, :width], current[:, width:]
    edge = half[:, : 2 * state_width]
    edge = edge + jnp.where(small, swap(lent), jnp.zeros_like(lent))
    return jnp.concatenate([edge, half[:, 2 * state_width :]], axis=1)


def paired_shards(
    stream,
    cotangent,
    positions,
    norm_gain,
    w_gate,
    w_inner,
    w_state,
    w_step,
    conv_inner,
    conv_state,
    head_params,
    gate_gain,
    w_out,
    moment_norm_gain,
    moment_w_gate,
    moment_w_inner,
    moment_w_state,
    moment_w_step,
    moment_conv_inner,
    moment_conv_state,
    moment_head_params,
    moment_gate_gain,
    moment_w_out,
):
    low = jnp.bfloat16
    core = lax.axis_index("tensor")
    room = w_gate.shape[1]
    wide = w_state.shape[1]
    col_width = wide // 2
    heads = w_step.shape[1]
    inv_first = lax.rsqrt(jnp.mean(stream * stream, axis=1, keepdims=True) + EPS)
    normed = (stream * inv_first * norm_gain).astype(low)
    first_pack = jnp.concatenate([w_gate.astype(low), w_state.astype(low)], axis=1)
    second_pack = jnp.concatenate([w_inner.astype(low), pad_cols(w_step.astype(low), 128)], axis=1)
    full_first = gather_rows(first_pack, (8, 4, 2, 1))
    full_second = gather_rows(second_pack, (8, 4, 1, 2))
    token_rows = pair_gather(normed)
    cotangent_rows = pair_gather(cotangent.astype(low))
    full_out = gather_rows(w_out.astype(low).T, (8, 4, 1, 2))
    first_pre = jnp.dot(token_rows, full_first, preferred_element_type=jnp.float32)
    second_pre = jnp.dot(token_rows, full_second, preferred_element_type=jnp.float32)
    gate_pre, state_pre = first_pre[:, :room], first_pre[:, room:]
    inner_pre, step_pre = second_pre[:, :room], second_pre[:, room : room + heads]
    alive = (positions >= 0).astype(jnp.float32)[:, None]
    scanned, core_back = jax.vjp(
        partial(mixer_core, positions=positions, precision=CORE),
        inner_pre,
        state_pre,
        step_pre,
        conv_inner,
        conv_state,
        head_params,
    )
    gate_act = jax.nn.silu(gate_pre)
    gated = scanned * gate_act
    square_part = jnp.sum(gated * gated, axis=1)
    d_normed_out = jnp.dot(cotangent_rows, full_out, preferred_element_type=jnp.float32)
    scaled = d_normed_out * gate_gain * alive
    cross_part = jnp.sum(scaled * gated, axis=1)
    sums = jnp.stack([square_part, cross_part])
    sums = sums + swap(sums)
    square_sum, cross_sum = sums[0], sums[1]
    inv_second = lax.rsqrt(square_sum / INNER + EPS)[:, None]
    normed_out = (gated * inv_second * gate_gain * alive).astype(low)
    mixed = pair_scatter(times_transpose(normed_out, full_out).astype(low), 0)
    output = stream + mixed
    grad_out_t = scatter_rows(contract_rows(cotangent_rows, normed_out).astype(low), (1, 2, 4, 8))
    grad_gate_part = jnp.sum(d_normed_out * gated * inv_second * alive, axis=0)
    d_gated = inv_second * scaled - gated * inv_second**3 * (cross_sum / INNER)[:, None]
    d_gate_pre = (d_gated * scanned * silu_slope(gate_pre)).astype(low)
    grad_gate_w = scatter_rows(contract_rows(token_rows, d_gate_pre).astype(low), (2, 1, 4, 8))
    d_inner, d_state_part, d_step, grad_conv_inner_part, grad_conv_state_part, grad_head_part = (
        core_back(d_gated * gate_act)
    )
    d_state_low = pair_scatter(d_state_part.astype(low), 1).astype(low)
    d_tail = jnp.concatenate(
        [d_inner.astype(low), d_state_low, pad_cols(d_step.astype(low), 128)], axis=1
    )
    col_first = core * col_width
    state_cols = lax.dynamic_slice_in_dim(full_first, room + col_first, col_width, 1)
    tail_weights = jnp.concatenate(
        [full_second[:, :room], state_cols, full_second[:, room:]], axis=1
    )
    total = times_transpose(d_gate_pre, full_first[:, :room])
    total = total + times_transpose(d_tail, tail_weights)
    d_normed = pair_scatter(total.astype(low), 0)
    tail_part = contract_rows(token_rows, d_tail).astype(low)
    cut = tail_part.shape[1] // 2
    tail_grad = jnp.concatenate(
        [
            scatter_rows(tail_part[:, :cut], (1, 2, 4, 8)),
            scatter_rows(tail_part[:, cut:], (2, 1, 4, 8)),
        ],
        axis=1,
    )
    grad_inner_w = tail_grad[:, :room]
    grad_state_w = tail_grad[:, room : room + col_width]
    grad_step_w = tail_grad[:, room + col_width : room + col_width + heads]
    grad_out_w = grad_out_t.T
    grad_norm_part = jnp.sum(d_normed * stream * inv_first, axis=0)
    weighted = d_normed * norm_gain
    d_stream = (
        cotangent
        + inv_first * weighted
        - stream * inv_first**3 * jnp.mean(weighted * stream, axis=1, keepdims=True)
    )
    shared = jnp.concatenate([grad_conv_state_part, grad_norm_part.reshape(-1, wide)], axis=0)
    shared = shared + swap(shared)
    vectors = jnp.concatenate(
        [
            grad_conv_inner_part,
            grad_gate_part[None, :],
            pad_cols(grad_head_part, room),
            pad_cols(shared, room),
        ],
        axis=0,
    )
    for bit in (1, 2, 4, 8):
        vectors = vectors + exchange(vectors, bit)
    grad_conv_inner = vectors[:5]
    grad_gate_gain = vectors[5]
    grad_head = vectors[6:9, :heads]
    grad_conv_state = vectors[9:14, :wide]
    grad_norm = vectors[14:, :wide].reshape(-1)
    m_gate = MU_MAT * moment_w_gate + grad_gate_w
    m_inner = MU_MAT * moment_w_inner + grad_inner_w
    m_state = MU_MAT * moment_w_state + grad_state_w
    m_step = MU_MAT * moment_w_step + grad_step_w
    m_out = MU_MAT * moment_w_out + grad_out_w
    small = pad_cols(jnp.concatenate([m_state, m_step], axis=1), room)
    tasks = jnp.stack([m_gate, m_inner, m_out.T, small]).astype(low)
    mine = from_owner(orthogonal_half(to_owner(tasks), col_width)).astype(jnp.float32)
    new_gate = w_gate - LR_MAT * spread(D, INNER) * mine[0]
    new_inner = w_inner - LR_MAT * spread(D, INNER) * mine[1]
    new_out = w_out - LR_MAT * spread(INNER, D) * mine[2].T
    new_step = w_step - LR_MAT * spread(D, HEADS) * mine[3][:, col_width : col_width + heads]
    state_slice = lax.dynamic_slice_in_dim(w_state, col_first, col_width, 1)
    new_state = state_slice - LR_MAT * spread(D, 2 * STATE) * mine[3][:, :col_width]
    m_norm = MU_VEC * moment_norm_gain + grad_norm
    m_conv_inner = MU_VEC * moment_conv_inner + grad_conv_inner
    m_conv_state = MU_VEC * moment_conv_state + grad_conv_state
    m_head = MU_VEC * moment_head_params + grad_head
    m_gate_gain = MU_VEC * moment_gate_gain + grad_gate_gain
    return (
        output,
        d_stream,
        grad_norm,
        grad_gate_w,
        grad_inner_w,
        grad_state_w,
        grad_step_w,
        grad_conv_inner,
        grad_conv_state,
        grad_head,
        grad_gate_gain,
        grad_out_w,
        norm_gain - LR_VEC * m_norm,
        new_gate,
        new_inner,
        new_state,
        new_step,
        conv_inner - LR_VEC * m_conv_inner,
        conv_state - LR_VEC * m_conv_state,
        head_params - LR_VEC * m_head,
        gate_gain - LR_VEC * m_gate_gain,
        new_out,
        m_norm,
        m_gate,
        m_inner,
        m_state,
        m_step,
        m_conv_inner,
        m_conv_state,
        m_head,
        m_gate_gain,
        m_out,
    )


def solution(mesh):
    paired = mesh.shape["dp"] == 16 and mesh.shape["tensor"] == 2
    return jax.shard_map(
        paired_shards if paired else shards,
        mesh=mesh,
        in_specs=(
            P(("dp", "tensor"), None),
            P(("dp", "tensor"), None),
            P("dp"),
            P(),
            P("dp", "tensor"),
            P("dp", "tensor"),
            P("dp", None),
            P("dp", "tensor"),
            P(None, "tensor"),
            P(),
            P(None, "tensor"),
            P("tensor"),
            P("tensor", "dp"),
            P(),
            P("dp", "tensor"),
            P("dp", "tensor"),
            P("dp", "tensor"),
            P("dp", "tensor"),
            P(None, "tensor"),
            P(),
            P(None, "tensor"),
            P("tensor"),
            P("tensor", "dp"),
        ),
        out_specs=(
            P(("dp", "tensor"), None),
            P(("dp", "tensor"), None),
            P(),
            P("dp", "tensor"),
            P("dp", "tensor"),
            P("dp", "tensor"),
            P("dp", "tensor"),
            P(None, "tensor"),
            P(),
            P(None, "tensor"),
            P("tensor"),
            P("tensor", "dp"),
            P(),
            P("dp", "tensor"),
            P("dp", "tensor"),
            P("dp", "tensor"),
            P("dp", "tensor"),
            P(None, "tensor"),
            P(),
            P(None, "tensor"),
            P("tensor"),
            P("tensor", "dp"),
            P(),
            P("dp", "tensor"),
            P("dp", "tensor"),
            P("dp", "tensor"),
            P("dp", "tensor"),
            P(None, "tensor"),
            P(),
            P(None, "tensor"),
            P("tensor"),
            P("tensor", "dp"),
        ),
        check_vma=False,
    )
```

```python
from functools import partial
import math

import jax
import jax.numpy as jnp
from jax import lax
from jax.sharding import PartitionSpec as P

D = 768
INNER = 1536
HEADS = 24
STATE = 128
BLOCK = 256
NS_STEPS = 5


EPS = 1e-05
NS_A = 3.4445
NS_B = -4.775
NS_C = 2.0315
MU_MAT = 0.95
MU_VEC = 0.9
LR_MAT = 0.3
LR_VEC = 0.001
HIGH = lax.Precision.HIGHEST
CORE = lax.Precision.DEFAULT


def silu_slope(value):
    sig = jax.nn.sigmoid(value)
    return sig * (1.0 + value * (1.0 - sig))


def contract_rows(left, right):
    return lax.dot_general(
        left, right, (((0,), (0,)), ((), ())), preferred_element_type=jnp.float32
    )


def times_transpose(left, right):
    return lax.dot_general(
        left, right, (((1,), (1,)), ((), ())), preferred_element_type=jnp.float32
    )


def causal_conv(signal, taps, positions):
    length = signal.shape[0]
    reach = taps.shape[0] - 1
    total = jnp.zeros_like(signal) + taps[reach]
    for lag_step in range(reach):
        moved = jnp.pad(signal, ((lag_step, 0), (0, 0)))[:length]
        total = total + jnp.where((positions >= lag_step)[:, None], moved * taps[lag_step], 0.0)
    return jax.nn.silu(total)


def mixer_core(inner_pre, state_pre, step_pre, conv_inner, conv_state, head_params, positions, precision=HIGH):
    length = inner_pre.shape[0]
    heads = step_pre.shape[1]
    head_size = inner_pre.shape[1] // heads
    states = state_pre.shape[1] // 2
    blocks = length // BLOCK
    inner_act = causal_conv(inner_pre, conv_inner, positions).reshape(
        blocks, BLOCK, heads, head_size
    )
    state_act = causal_conv(state_pre, conv_state, positions)
    input_map = state_act[:, :states].reshape(blocks, BLOCK, states)
    output_map = state_act[:, states:].reshape(blocks, BLOCK, states)
    step_size = jax.nn.softplus(step_pre + head_params[0])
    log_decay = (step_size * -jnp.exp(head_params[1])).reshape(blocks, BLOCK, heads)
    step_size = step_size.reshape(blocks, BLOCK, heads)
    resets = (positions <= 0).astype(jnp.float32).reshape(blocks, BLOCK)
    order = jnp.arange(BLOCK)
    lower = (order[:, None] >= order[None, :]).astype(jnp.float32)
    cumulative = jnp.einsum("ij,cjh->cih", lower, log_decay, precision=HIGH)
    seen = jnp.einsum("ij,cj->ci", lower, resets, precision=HIGH)
    linked = (seen[:, :, None] == seen[:, None, :]) & (order[:, None] >= order[None, :])[None]
    linked_heads = linked[..., None]
    spacing = cumulative[:, :, None, :] - cumulative[:, None, :, :]
    decay = jnp.where(linked_heads, jnp.exp(jnp.where(linked_heads, spacing, 0.0)), 0.0)
    scores = jnp.einsum("cin,cjn->cij", output_map, input_map, precision=precision)
    mixing = scores[..., None] * decay * step_size[:, None, :, :]
    within = jnp.einsum("cijh,cjhp->cihp", mixing, inner_act, precision=precision)
    tail_linked = (seen[:, -1:] == seen)[..., None]
    tail = (
        jnp.where(
            tail_linked,
            jnp.exp(jnp.where(tail_linked, cumulative[:, -1:, :] - cumulative, 0.0)),
            0.0,
        )
        * step_size
    )
    own_state = jnp.einsum("cjh,cjhp,cjn->chpn", tail, inner_act, input_map, precision=precision)
    carry_rate = jnp.exp(cumulative[:, -1, :]) * (seen[:, -1] == 0).astype(jnp.float32)[:, None]

    state = jnp.zeros((heads, head_size, states), jnp.float32)
    entering = []
    for block in range(blocks):
        entering.append(state)
        state = carry_rate[block][:, None, None] * state + own_state[block]
    entering = jnp.stack(entering)
    fresh = (seen == 0)[..., None]
    carry_in = jnp.where(fresh, jnp.exp(cumulative), 0.0)
    across = (
        jnp.einsum("cin,chpn->cihp", output_map, entering, precision=precision) * carry_in[..., None]
    )
    result = within + across + head_params[2][None, None, :, None] * inner_act
    return result.reshape(length, heads * head_size)


def gram_total(low):
    return lax.psum(
        jnp.dot(low, low.T, preferred_element_type=jnp.float32).astype(jnp.bfloat16), "tensor"
    ).astype(jnp.float32)


def orthogonalize(matrix):
    first = gram_total(matrix.astype(jnp.bfloat16))
    scale = jnp.sqrt(jnp.trace(first)) + 1e-07
    current = (matrix / scale).astype(jnp.bfloat16)
    gram = (first / (scale * scale)).astype(jnp.bfloat16)
    for turn in range(NS_STEPS):
        if turn > 0:
            gram = gram_total(current).astype(jnp.bfloat16)
        applied = jnp.dot(gram, current, preferred_element_type=jnp.float32)
        twice = jnp.dot(gram, applied.astype(jnp.bfloat16), preferred_element_type=jnp.float32)
        current = (NS_A * current.astype(jnp.float32) + NS_B * applied + NS_C * twice).astype(
            jnp.bfloat16
        )
    return current.astype(jnp.float32)


def spread(rows, cols):
    return math.sqrt(max(1.0, rows / cols))


def shards(
    stream,
    cotangent,
    positions,
    norm_gain,
    w_gate,
    w_inner,
    w_state,
    w_step,
    conv_inner,
    conv_state,
    head_params,
    gate_gain,
    w_out,
    moment_norm_gain,
    moment_w_gate,
    moment_w_inner,
    moment_w_state,
    moment_w_step,
    moment_conv_inner,
    moment_conv_state,
    moment_head_params,
    moment_gate_gain,
    moment_w_out,
):
    dp_count = lax.axis_size("dp")
    inv_first = lax.rsqrt(jnp.mean(stream * stream, axis=1, keepdims=True) + EPS)
    normed = (stream * inv_first * norm_gain).astype(jnp.bfloat16)
    token_rows, cotangent_rows = (
        lax.all_gather(normed, "tensor", axis=0, tiled=True),
        lax.all_gather(cotangent.astype(jnp.bfloat16), "tensor", axis=0, tiled=True),
    )
    local_weights = (
        w_gate.astype(jnp.bfloat16),
        w_inner.astype(jnp.bfloat16),
        w_step.astype(jnp.bfloat16),
        w_state.astype(jnp.bfloat16),
        w_out.astype(jnp.bfloat16),
    )
    full_gate, full_inner, full_step, full_state, full_out = (
        lax.all_gather(local_weights[0], "dp", axis=0, tiled=True),
        lax.all_gather(local_weights[1], "dp", axis=0, tiled=True),
        lax.all_gather(local_weights[2], "dp", axis=0, tiled=True),
        lax.all_gather(local_weights[3], "dp", axis=0, tiled=True),
        lax.all_gather(local_weights[4], "dp", axis=1, tiled=True),
    )
    gate_pre = jnp.dot(token_rows, full_gate, preferred_element_type=jnp.float32)
    inner_pre = jnp.dot(token_rows, full_inner, preferred_element_type=jnp.float32)
    state_pre = jnp.dot(token_rows, full_state, preferred_element_type=jnp.float32)
    step_pre = jnp.dot(token_rows, full_step, preferred_element_type=jnp.float32)
    alive = (positions >= 0).astype(jnp.float32)[:, None]
    scanned, core_back = jax.vjp(
        partial(mixer_core, positions=positions),
        inner_pre,
        state_pre,
        step_pre,
        conv_inner,
        conv_state,
        head_params,
    )
    gate_act = jax.nn.silu(gate_pre)
    gated = scanned * gate_act
    square_sum = lax.psum(jnp.sum(gated * gated, axis=1), "tensor")
    inv_second = lax.rsqrt(square_sum / INNER + EPS)[:, None]
    normed_out = (gated * inv_second * gate_gain * alive).astype(jnp.bfloat16)
    mixed = lax.psum_scatter(
        jnp.dot(normed_out, full_out, preferred_element_type=jnp.float32).astype(jnp.bfloat16),
        "tensor",
        scatter_dimension=0,
        tiled=True,
    ).astype(jnp.float32)
    output = stream + mixed
    d_normed_out = times_transpose(cotangent_rows, full_out)
    grad_out_part = contract_rows(normed_out, cotangent_rows)
    scaled = d_normed_out * gate_gain * alive
    grad_gate_part = jnp.sum(d_normed_out * gated * inv_second * alive, axis=0)
    cross_sum = lax.psum(jnp.sum(scaled * gated, axis=1), "tensor")
    d_gated = inv_second * scaled - gated * inv_second**3 * (cross_sum / INNER)[:, None]
    d_gate_pre = (d_gated * scanned * silu_slope(gate_pre)).astype(jnp.bfloat16)
    d_inner, d_state_part, d_step, grad_conv_inner_part, grad_conv_state_part, grad_head_part = (
        core_back(d_gated * gate_act)
    )
    d_state_cols = lax.psum_scatter(
        d_state_part.astype(jnp.bfloat16), "tensor", scatter_dimension=1, tiled=True
    ).astype(jnp.float32)
    d_inner_low = d_inner.astype(jnp.bfloat16)
    d_state_low = d_state_cols.astype(jnp.bfloat16)
    d_step_low = d_step.astype(jnp.bfloat16)
    col_width = d_state_cols.shape[1]
    col_first = lax.axis_index("tensor") * col_width
    state_cols = lax.dynamic_slice_in_dim(full_state, col_first, col_width, 1)
    total = times_transpose(d_gate_pre, full_gate)
    total = total + times_transpose(d_inner_low, full_inner)
    total = total + times_transpose(d_state_low, state_cols)
    d_normed = lax.psum_scatter(
        (total + times_transpose(d_step_low, full_step)).astype(jnp.bfloat16),
        "tensor",
        scatter_dimension=0,
        tiled=True,
    ).astype(jnp.float32)
    grad_gate_w, grad_inner_w, grad_state_w, grad_step_w, grad_out_w = (
        lax.psum_scatter(
            contract_rows(token_rows, d_gate_pre).astype(jnp.bfloat16),
            "dp",
            scatter_dimension=0,
            tiled=True,
        ).astype(jnp.float32),
        lax.psum_scatter(
            contract_rows(token_rows, d_inner_low).astype(jnp.bfloat16),
            "dp",
            scatter_dimension=0,
            tiled=True,
        ).astype(jnp.float32),
        lax.psum_scatter(
            contract_rows(token_rows, d_state_low).astype(jnp.bfloat16),
            "dp",
            scatter_dimension=0,
            tiled=True,
        ).astype(jnp.float32),
        lax.psum_scatter(
            contract_rows(token_rows, d_step_low).astype(jnp.bfloat16),
            "dp",
            scatter_dimension=0,
            tiled=True,
        ).astype(jnp.float32),
        lax.psum_scatter(
            grad_out_part.astype(jnp.bfloat16), "dp", scatter_dimension=1, tiled=True
        ).astype(jnp.float32),
    )
    grad_norm_part = jnp.sum(d_normed * stream * inv_first, axis=0)
    weighted = d_normed * norm_gain
    d_stream = (
        cotangent
        + inv_first * weighted
        - stream * inv_first**3 * jnp.mean(weighted * stream, axis=1, keepdims=True)
    )
    grad_conv_inner, grad_gate_gain, grad_head = lax.psum(
        (grad_conv_inner_part, grad_gate_part, grad_head_part), "dp"
    )
    grad_conv_state, grad_norm = lax.psum((grad_conv_state_part, grad_norm_part), ("dp", "tensor"))
    m_gate = MU_MAT * moment_w_gate + grad_gate_w
    m_inner = MU_MAT * moment_w_inner + grad_inner_w
    m_state = MU_MAT * moment_w_state + grad_state_w
    m_step = MU_MAT * moment_w_step + grad_step_w
    m_out = MU_MAT * moment_w_out + grad_out_w
    room = w_gate.shape[1]
    shard_rows = w_gate.shape[0]
    stacked = jnp.stack(
        [
            m_gate,
            m_inner,
            m_out.T,
            jnp.pad(m_step, ((0, 0), (0, room - m_step.shape[1]))),
            jnp.pad(m_state, ((0, 0), (0, room - m_state.shape[1]))),
        ]
    )
    matrix_count = stacked.shape[0]
    owner_index = jnp.arange(matrix_count, dtype=jnp.int32) * dp_count // matrix_count
    select = (owner_index[None, :] == jnp.arange(dp_count, dtype=jnp.int32)[:, None]).astype(
        jnp.float32
    )
    outgoing = jnp.einsum("jk,krc->jrc", select, stacked, precision=HIGH)
    owned = (
        lax.all_to_all(outgoing.astype(jnp.bfloat16), "dp", split_axis=0, concat_axis=0, tiled=True)
        .astype(outgoing.dtype)
        .reshape(dp_count * shard_rows, room)
    )
    ortho = orthogonalize(owned)
    returned = lax.all_to_all(
        ortho.reshape(dp_count, shard_rows, room).astype(jnp.bfloat16),
        "dp",
        split_axis=0,
        concat_axis=0,
        tiled=True,
    ).astype(jnp.float32)
    mine = jnp.einsum("jk,jrc->krc", select, returned, precision=HIGH)
    new_gate = w_gate - LR_MAT * spread(D, INNER) * mine[0]
    new_inner = w_inner - LR_MAT * spread(D, INNER) * mine[1]
    new_out = w_out - LR_MAT * spread(INNER, D) * mine[2].T
    new_step = w_step - LR_MAT * spread(D, HEADS) * mine[3][:, : w_step.shape[1]]
    state_slice = lax.dynamic_slice_in_dim(w_state, col_first, col_width, 1)
    new_state = state_slice - LR_MAT * spread(D, 2 * STATE) * mine[4][:, :col_width]
    m_norm = MU_VEC * moment_norm_gain + grad_norm
    m_conv_inner = MU_VEC * moment_conv_inner + grad_conv_inner
    m_conv_state = MU_VEC * moment_conv_state + grad_conv_state
    m_head = MU_VEC * moment_head_params + grad_head
    m_gate_gain = MU_VEC * moment_gate_gain + grad_gate_gain
    return (
        output,
        d_stream,
        grad_norm,
        grad_gate_w,
        grad_inner_w,
        grad_state_w,
        grad_step_w,
        grad_conv_inner,
        grad_conv_state,
        grad_head,
        grad_gate_gain,
        grad_out_w,
        norm_gain - LR_VEC * m_norm,
        new_gate,
        new_inner,
        new_state,
        new_step,
        conv_inner - LR_VEC * m_conv_inner,
        conv_state - LR_VEC * m_conv_state,
        head_params - LR_VEC * m_head,
        gate_gain - LR_VEC * m_gate_gain,
        new_out,
        m_norm,
        m_gate,
        m_inner,
        m_state,
        m_step,
        m_conv_inner,
        m_conv_state,
        m_head,
        m_gate_gain,
        m_out,
    )


def exchange(value, bit):
    count = lax.axis_size("dp")
    return lax.ppermute(value, "dp", [(i, i ^ bit) for i in range(count)])


def swap(value):
    return lax.ppermute(value, "tensor", [(0, 1), (1, 0)])


def bit_of(bit):
    return (lax.axis_index("dp") // bit) % 2


def join(kept, received, mine, axis):
    first = jnp.where(mine == 0, kept, received)
    second = jnp.where(mine == 0, received, kept)
    return jnp.concatenate([first, second], axis=axis)


AXIS_OF = {8: 0, 4: 1, 2: 2, 1: 3}


def spread_rows(held, order):
    for bit in order:
        held = join(held, exchange(held, bit), bit_of(bit), AXIS_OF[bit])
    return held


def gather_rows(block, order):
    rows, cols = block.shape
    held = spread_rows(block.reshape(1, 1, 1, 1, rows, cols), order)
    return held.reshape(16 * rows, cols)


def scatter_rows(part, order):
    rows, cols = part.shape
    held = part.reshape(2, 2, 2, 2, rows // 16, cols)
    for bit in order:
        axis = AXIS_OF[bit]
        mine = bit_of(bit)
        send = lax.dynamic_index_in_dim(held, 1 - mine, axis, keepdims=True)
        keep = lax.dynamic_index_in_dim(held, mine, axis, keepdims=True)
        total = keep.astype(jnp.float32) + exchange(send.astype(jnp.bfloat16), bit).astype(
            jnp.float32
        )
        held = total.astype(jnp.bfloat16) if bit != order[-1] else total
    return held.reshape(rows // 16, cols)


def pair_gather(block):
    return join(block, swap(block), lax.axis_index("tensor"), 0)


def pair_scatter(part, axis):
    mine = lax.axis_index("tensor")
    width = part.shape[axis] // 2
    keep = lax.dynamic_slice_in_dim(part, mine * width, width, axis)
    send = lax.dynamic_slice_in_dim(part, (1 - mine) * width, width, axis)
    return keep.astype(jnp.float32) + swap(send.astype(jnp.bfloat16)).astype(jnp.float32)


def pad_cols(value, width):
    return jnp.pad(value, ((0, 0), (0, width - value.shape[1])))


def to_owner(tasks):
    _, rows, cols = tasks.shape
    across, along = bit_of(1), bit_of(2)
    held = tasks.reshape(2, 2, rows, cols)
    send = lax.dynamic_index_in_dim(held, 1 - across, 1)
    keep = lax.dynamic_index_in_dim(held, across, 1)
    held = join(keep, exchange(send, 1), across, 1)
    send = lax.dynamic_index_in_dim(held, 1 - along, 0)
    keep = lax.dynamic_index_in_dim(held, along, 0)
    held = join(keep, exchange(send, 2), along, 0)
    held = spread_rows(held.reshape(1, 1, 2, 2, rows, cols), (8, 4))
    return held.reshape(16 * rows, cols)


def from_owner(matrix):
    rows, cols = matrix.shape[0] // 16, matrix.shape[1]
    across, along = bit_of(1), bit_of(2)
    plane = lax.dynamic_index_in_dim(
        matrix.reshape(4, 2, 2, rows, cols), lax.axis_index("dp") // 4, 0, keepdims=False
    )
    send = lax.dynamic_index_in_dim(plane, 1 - along, 0)
    keep = lax.dynamic_index_in_dim(plane, along, 0)
    held = join(keep, exchange(send, 2), along, 0)
    send = lax.dynamic_index_in_dim(held, 1 - across, 1)
    keep = lax.dynamic_index_in_dim(held, across, 1)
    return join(keep, exchange(send, 1), across, 1).reshape(4, rows, cols)


def orthogonal_half(own, state_width):
    width = own.shape[1]
    small = lax.axis_index("dp") % 4 == 3
    full = jnp.concatenate([own, swap(own)], axis=1)
    col = jnp.arange(2 * width)[None, :] % width
    keep = (col < state_width) == (lax.axis_index("tensor") == 0)
    full = jnp.where(small & ~keep, jnp.zeros_like(full), full)
    first = times_transpose(full, full)
    scale = jnp.sqrt(jnp.sum(jnp.square(full.astype(jnp.float32)))) + 1e-07
    current = (full.astype(jnp.float32) / scale).astype(jnp.bfloat16)
    gram = (first / (scale * scale)).astype(jnp.bfloat16)
    for turn in range(NS_STEPS):
        if turn > 0:
            gram = times_transpose(current, current).astype(jnp.bfloat16)
        square = jnp.dot(gram, gram, preferred_element_type=jnp.float32)
        mix = (NS_B * gram.astype(jnp.float32) + NS_C * square).astype(jnp.bfloat16)
        if turn == NS_STEPS - 1:
            current = current[:, : width + 2 * state_width]
        current = (
            NS_A * current.astype(jnp.float32)
            + jnp.dot(mix, current, preferred_element_type=jnp.float32)
        ).astype(jnp.bfloat16)
    half, lent = current[:, :width], current[:, width:]
    edge = half[:, : 2 * state_width]
    edge = edge + jnp.where(small, swap(lent), jnp.zeros_like(lent))
    return jnp.concatenate([edge, half[:, 2 * state_width :]], axis=1)


def paired_shards(
    stream,
    cotangent,
    positions,
    norm_gain,
    w_gate,
    w_inner,
    w_state,
    w_step,
    conv_inner,
    conv_state,
    head_params,
    gate_gain,
    w_out,
    moment_norm_gain,
    moment_w_gate,
    moment_w_inner,
    moment_w_state,
    moment_w_step,
    moment_conv_inner,
    moment_conv_state,
    moment_head_params,
    moment_gate_gain,
    moment_w_out,
):
    low = jnp.bfloat16
    core = lax.axis_index("tensor")
    room = w_gate.shape[1]
    wide = w_state.shape[1]
    col_width = wide // 2
    heads = w_step.shape[1]
    inv_first = lax.rsqrt(jnp.mean(stream * stream, axis=1, keepdims=True) + EPS)
    normed = (stream * inv_first * norm_gain).astype(low)
    first_pack = jnp.concatenate([w_gate.astype(low), w_state.astype(low)], axis=1)
    second_pack = jnp.concatenate([w_inner.astype(low), pad_cols(w_step.astype(low), 128)], axis=1)
    full_first = gather_rows(first_pack, (8, 4, 2, 1))
    full_second = gather_rows(second_pack, (8, 4, 1, 2))
    token_rows = pair_gather(normed)
    cotangent_rows = pair_gather(cotangent.astype(low))
    full_out = gather_rows(w_out.astype(low).T, (8, 4, 1, 2))
    first_pre = jnp.dot(token_rows, full_first, preferred_element_type=jnp.float32)
    second_pre = jnp.dot(token_rows, full_second, preferred_element_type=jnp.float32)
    gate_pre, state_pre = first_pre[:, :room], first_pre[:, room:]
    inner_pre, step_pre = second_pre[:, :room], second_pre[:, room : room + heads]
    alive = (positions >= 0).astype(jnp.float32)[:, None]
    scanned, core_back = jax.vjp(
        partial(mixer_core, positions=positions, precision=CORE),
        inner_pre,
        state_pre,
        step_pre,
        conv_inner,
        conv_state,
        head_params,
    )
    gate_act = jax.nn.silu(gate_pre)
    gated = scanned * gate_act
    square_part = jnp.sum(gated * gated, axis=1)
    d_normed_out = jnp.dot(cotangent_rows, full_out, preferred_element_type=jnp.float32)
    scaled = d_normed_out * gate_gain * alive
    cross_part = jnp.sum(scaled * gated, axis=1)
    sums = jnp.stack([square_part, cross_part])
    sums = sums + swap(sums)
    square_sum, cross_sum = sums[0], sums[1]
    inv_second = lax.rsqrt(square_sum / INNER + EPS)[:, None]
    normed_out = (gated * inv_second * gate_gain * alive).astype(low)
    mixed = pair_scatter(times_transpose(normed_out, full_out).astype(low), 0)
    output = stream + mixed
    grad_out_t = scatter_rows(contract_rows(cotangent_rows, normed_out).astype(low), (1, 2, 4, 8))
    grad_gate_part = jnp.sum(d_normed_out * gated * inv_second * alive, axis=0)
    d_gated = inv_second * scaled - gated * inv_second**3 * (cross_sum / INNER)[:, None]
    d_gate_pre = (d_gated * scanned * silu_slope(gate_pre)).astype(low)
    grad_gate_w = scatter_rows(contract_rows(token_rows, d_gate_pre).astype(low), (2, 1, 4, 8))
    d_inner, d_state_part, d_step, grad_conv_inner_part, grad_conv_state_part, grad_head_part = (
        core_back(d_gated * gate_act)
    )
    d_state_low = pair_scatter(d_state_part.astype(low), 1).astype(low)
    d_tail = jnp.concatenate(
        [d_inner.astype(low), d_state_low, pad_cols(d_step.astype(low), 128)], axis=1
    )
    col_first = core * col_width
    state_cols = lax.dynamic_slice_in_dim(full_first, room + col_first, col_width, 1)
    tail_weights = jnp.concatenate(
        [full_second[:, :room], state_cols, full_second[:, room:]], axis=1
    )
    total = times_transpose(d_gate_pre, full_first[:, :room])
    total = total + times_transpose(d_tail, tail_weights)
    d_normed = pair_scatter(total.astype(low), 0)
    tail_part = contract_rows(token_rows, d_tail).astype(low)
    cut = tail_part.shape[1] // 2
    tail_grad = jnp.concatenate(
        [
            scatter_rows(tail_part[:, :cut], (1, 2, 4, 8)),
            scatter_rows(tail_part[:, cut:], (2, 1, 4, 8)),
        ],
        axis=1,
    )
    grad_inner_w = tail_grad[:, :room]
    grad_state_w = tail_grad[:, room : room + col_width]
    grad_step_w = tail_grad[:, room + col_width : room + col_width + heads]
    grad_out_w = grad_out_t.T
    grad_norm_part = jnp.sum(d_normed * stream * inv_first, axis=0)
    weighted = d_normed * norm_gain
    d_stream = (
        cotangent
        + inv_first * weighted
        - stream * inv_first**3 * jnp.mean(weighted * stream, axis=1, keepdims=True)
    )
    shared = jnp.concatenate([grad_conv_state_part, grad_norm_part.reshape(-1, wide)], axis=0)
    shared = shared + swap(shared)
    vectors = jnp.concatenate(
        [
            grad_conv_inner_part,
            grad_gate_part[None, :],
            pad_cols(grad_head_part, room),
            pad_cols(shared, room),
        ],
        axis=0,
    )
    for bit in (1, 2, 4, 8):
        vectors = vectors + exchange(vectors, bit)
    grad_conv_inner = vectors[:5]
    grad_gate_gain = vectors[5]
    grad_head = vectors[6:9, :heads]
    grad_conv_state = vectors[9:14, :wide]
    grad_norm = vectors[14:, :wide].reshape(-1)
    m_gate = MU_MAT * moment_w_gate + grad_gate_w
    m_inner = MU_MAT * moment_w_inner + grad_inner_w
    m_state = MU_MAT * moment_w_state + grad_state_w
    m_step = MU_MAT * moment_w_step + grad_step_w
    m_out = MU_MAT * moment_w_out + grad_out_w
    small = pad_cols(jnp.concatenate([m_state, m_step], axis=1), room)
    tasks = jnp.stack([m_gate, m_inner, m_out.T, small]).astype(low)
    mine = from_owner(orthogonal_half(to_owner(tasks), col_width)).astype(jnp.float32)
    new_gate = w_gate - LR_MAT * spread(D, INNER) * mine[0]
    new_inner = w_inner - LR_MAT * spread(D, INNER) * mine[1]
    new_out = w_out - LR_MAT * spread(INNER, D) * mine[2].T
    new_step = w_step - LR_MAT * spread(D, HEADS) * mine[3][:, col_width : col_width + heads]
    state_slice = lax.dynamic_slice_in_dim(w_state, col_first, col_width, 1)
    new_state = state_slice - LR_MAT * spread(D, 2 * STATE) * mine[3][:, :col_width]
    m_norm = MU_VEC * moment_norm_gain + grad_norm
    m_conv_inner = MU_VEC * moment_conv_inner + grad_conv_inner
    m_conv_state = MU_VEC * moment_conv_state + grad_conv_state
    m_head = MU_VEC * moment_head_params + grad_head
    m_gate_gain = MU_VEC * moment_gate_gain + grad_gate_gain
    return (
        output,
        d_stream,
        grad_norm,
        grad_gate_w,
        grad_inner_w,
        grad_state_w,
        grad_step_w,
        grad_conv_inner,
        grad_conv_state,
        grad_head,
        grad_gate_gain,
        grad_out_w,
        norm_gain - LR_VEC * m_norm,
        new_gate,
        new_inner,
        new_state,
        new_step,
        conv_inner - LR_VEC * m_conv_inner,
        conv_state - LR_VEC * m_conv_state,
        head_params - LR_VEC * m_head,
        gate_gain - LR_VEC * m_gate_gain,
        new_out,
        m_norm,
        m_gate,
        m_inner,
        m_state,
        m_step,
        m_conv_inner,
        m_conv_state,
        m_head,
        m_gate_gain,
        m_out,
    )


def solution(mesh):
    paired = mesh.shape["dp"] == 16 and mesh.shape["tensor"] == 2
    return jax.shard_map(
        paired_shards if paired else shards,
        mesh=mesh,
        in_specs=(
            P(("dp", "tensor"), None),
            P(("dp", "tensor"), None),
            P("dp"),
            P(),
            P("dp", "tensor"),
            P("dp", "tensor"),
            P("dp", None),
            P("dp", "tensor"),
            P(None, "tensor"),
            P(),
            P(None, "tensor"),
            P("tensor"),
            P("tensor", "dp"),
            P(),
            P("dp", "tensor"),
            P("dp", "tensor"),
            P("dp", "tensor"),
            P("dp", "tensor"),
            P(None, "tensor"),
            P(),
            P(None, "tensor"),
            P("tensor"),
            P("tensor", "dp"),
        ),
        out_specs=(
            P(("dp", "tensor"), None),
            P(("dp", "tensor"), None),
            P(),
            P("dp", "tensor"),
            P("dp", "tensor"),
            P("dp", "tensor"),
            P("dp", "tensor"),
            P(None, "tensor"),
            P(),
            P(None, "tensor"),
            P("tensor"),
            P("tensor", "dp"),
            P(),
            P("dp", "tensor"),
            P("dp", "tensor"),
            P("dp", "tensor"),
            P("dp", "tensor"),
            P(None, "tensor"),
            P(),
            P(None, "tensor"),
            P("tensor"),
            P("tensor", "dp"),
            P(),
            P("dp", "tensor"),
            P("dp", "tensor"),
            P("dp", "tensor"),
            P("dp", "tensor"),
            P(None, "tensor"),
            P(),
            P(None, "tensor"),
            P("tensor"),
            P("tensor", "dp"),
        ),
        check_vma=False,
    )
```
